32 devices in a mesh: dp: 4 (over z), section: 2 (over core), ctx: 4 (over y, x).
Axes of the slice: x: 2, y: 2, z: 4, core: 2. Of those that a mesh axis runs over, the one named last changes fastest.
Arguments:
- features: bfloat16 [2, 4096, 8192], P('section', 'ctx', 'dp'), may hold values from -6 to 6
- queries: bfloat16 [2, 4096, 8192], P('section', 'ctx', 'dp'), may hold values from -6 to 6
- keys: bfloat16 [2, 4096, 1024], P('section', 'ctx', 'dp'), may hold values from -6 to 6
- values: bfloat16 [2, 4096, 1024], P('section', 'ctx', 'dp'), may hold values from -6 to 6
- attn_out: bfloat16 [2, 4096, 8192], P('section', 'ctx', 'dp'), may hold values from -4 to 4
- out_grad: bfloat16 [2, 4096, 8192], P('section', 'ctx', 'dp'), may hold values from -6 to 6
- lse: float32 [2, 64, 4096], P('section', 'dp', 'ctx'), as said below
- doc_starts: int32 [2, 65], P('section'), may hold values from 0 to 4096, as said below
- key_blocks: int32 [2, 32, 17], P('section', 'ctx'), may hold values from -1 to 31, as said below
Outputs:
- query_grad: bfloat16 [2, 4096, 8192], P('section', 'ctx', 'dp')
- key_grad: bfloat16 [2, 4096, 1024], P('section', 'ctx', 'dp')
- value_grad: bfloat16 [2, 4096, 1024], P('section', 'ctx', 'dp')
- value_weight_grad: float32 [2, 8192, 1024], P('section', ('dp', 'ctx'))
The draws below stay inside these ranges and needn't reach their ends.
Inputs may be any that keep to these rules, and one draw needn't show every extreme that they name: `doc_starts`: each row lists the first token of each document of one sequence, rising from 0; entries after the last document equal 4096. Every document has 64 to 2049 tokens, except the last, which the sequence's end may cut shorter; one of the first two documents of every sequence has exactly 2049 tokens. `key_blocks`: row b of a section (query block b of 128 tokens) lists in rising order the key blocks from the block holding the start of the document of block b's first token up to b itself, then -1 in the remaining entries. Every section has a row with all 17 entries used. `lse`: Non-negative.
All inputs are finite; a program needn't handle non-finite values.
Results may differ from the reference program's by a relative error of at most 0.0065.
Values may be sent and summed in bfloat16 or wider, within the bound.
A program may use at most 128 MiB of HBM per device.

```python
import jax
import jax.numpy as jnp
from jax import lax

DW = 8192
QH = 64
KVH = 8
HD = 128
DOC_LEAST = 64
QW = 8192
KVW = 1024
SECTIONS = 2
SEQ = 4096
NBLK = 32
KMAX = 17
DOC_MOST = 2049
DOC_CAP = 65


def doc_layout(key):
    base_key = jax.random.fold_in(key, 7)
    seq_keys = jax.random.split(base_key, SECTIONS)

    def one_sequence(seq_key):
        len_key, flag_key, first_key = jax.random.split(seq_key, 3)
        lengths = jax.random.randint(len_key, (DOC_CAP,), DOC_LEAST, DOC_MOST + 1)
        forced_second = jax.random.randint(flag_key, (), 0, 2)
        first_length = jax.random.randint(first_key, (), DOC_LEAST, min(DOC_MOST, SEQ - DOC_MOST) + 1)
        lengths = lengths.at[0].set(jnp.where(forced_second == 1, first_length, DOC_MOST))
        lengths = lengths.at[1].set(jnp.where(forced_second == 1, DOC_MOST, lengths[1]))
        doc_ends = jnp.cumsum(lengths).astype(jnp.int32)
        starts = jnp.concatenate([jnp.zeros((1,), jnp.int32), doc_ends[:-1]])
        return jnp.minimum(starts, SEQ).astype(jnp.int32)
    return jax.vmap(one_sequence)(seq_keys).reshape(SECTIONS, DOC_CAP)


def begin_of_doc(starts, positions):
    hits = starts[:, None, :] <= positions[None, :, None]
    return jnp.max(jnp.where(hits, starts[:, None, :], 0), axis=-1)


def draw_doc_starts(key, part):
    return doc_layout(key)


def draw_key_blocks(key, part):
    starts = doc_layout(key)
    block_ids = jnp.arange(NBLK, dtype=jnp.int32)
    doc_begin = begin_of_doc(starts, block_ids * 128)
    entries = (doc_begin // 128)[..., None] + jnp.arange(KMAX, dtype=jnp.int32)
    listed = jnp.where(entries <= block_ids[None, :, None], entries, -1)
    return listed.reshape(SECTIONS, NBLK, KMAX).astype(jnp.int32)


def draw_lse(key, part):
    starts = doc_layout(key)
    positions = jnp.arange(SEQ, dtype=jnp.int32)
    doc_begin = begin_of_doc(starts, positions)
    visible = (positions[None, :] - doc_begin + 1).astype(jnp.float32)
    base_part = jnp.log(visible).reshape(SECTIONS, 1, SEQ)
    noise_key = jax.random.fold_in(key, 11)
    offset = jax.random.uniform(noise_key, (SECTIONS, QH, SEQ), jnp.float32, 0.3, 0.8)
    return (base_part + offset).astype(jnp.float32)


def spiked(values, rng, source, target, shards_of, factor):
    owner, partner = [(jnp.arange(values.shape[dim]) // (values.shape[dim] // shards_of)).reshape([-1 if axis == dim else 1 for axis in range(values.ndim)]) for dim in (source, target)]
    chosen = jax.random.permutation(rng, shards_of)[partner]
    strong = (owner == chosen) | (owner == (partner + shards_of // 2) % shards_of)
    return jnp.where(strong, factor * values, values)


def block_levels(key, dims, pieces, least, high):
    gain = 1.0
    for axis_at, blocks in pieces:
        draws = jax.random.uniform(jax.random.fold_in(jax.random.fold_in(key, 6), axis_at), (blocks,), jnp.float32, least / len(pieces), high / len(pieces))
        gain = gain * jnp.repeat(jnp.exp(draws), dims[axis_at] // blocks).reshape((-1,) + (1,) * (len(dims) - 1 - axis_at))
    return gain


def scatter_about(key, shape, scale, bound, cuts=(), kind=jnp.bfloat16):
    values = jax.random.normal(key, shape, jnp.float32) * scale
    if len(cuts) > 0:
        values = block_levels(key, shape, cuts, -0.22, 0.18) * values
    return jnp.clip(values, min=-bound, max=bound).astype(kind)


def gaussian_with(key, extent, deviation, limit, pieces, heavy, held_as=jnp.bfloat16):
    values = deviation * jax.random.normal(key, extent, jnp.float32)
    if pieces:
        values = values * block_levels(key, extent, pieces, -0.22, 0.18)
    return jnp.clip(spiked(values, jax.random.fold_in(key, 3), *heavy), -limit, limit).astype(held_as)


def setup_inputs(seed: int = 0) -> dict:
    streams_of = jax.random.split(jax.random.key(seed), 10)
    features = gaussian_with(streams_of[0], (SECTIONS, SEQ, DW), 1.0, 6.0, ((0, 2), (1, 4), (2, 4)), (1, 2, 4, 2.0))
    queries = scatter_about(streams_of[1], (SECTIONS, SEQ, QW), 1.0, 6.0, ((0, 2), (1, 4), (2, 4)))
    keys = scatter_about(streams_of[2], (SECTIONS, SEQ, KVW), 1.0, 6.0, ((0, 2), (1, 4), (2, 4)))
    values = scatter_about(streams_of[3], (SECTIONS, SEQ, KVW), 1.0, 6.0, ((0, 2), (1, 4), (2, 4)))
    attn_out = scatter_about(streams_of[4], (SECTIONS, SEQ, QW), 0.3, 4.0, ((0, 2), (1, 4), (2, 4)))
    out_grad = scatter_about(streams_of[5], (SECTIONS, SEQ, QW), 1.0, 6.0, ((0, 2), (1, 4), (2, 4)))
    lse = draw_lse(jax.random.fold_in(streams_of[9], 71), 0)
    doc_starts = draw_doc_starts(jax.random.fold_in(streams_of[9], 71), 0)
    key_blocks = draw_key_blocks(jax.random.fold_in(streams_of[9], 71), 0)
    return {"features": features, "queries": queries, "keys": keys, "values": values, "attn_out": attn_out, "out_grad": out_grad, "lse": lse, "doc_starts": doc_starts, "key_blocks": key_blocks}


def doc_index(starts, positions):
    return jnp.sum((starts[None, :] <= positions[:, None]).astype(jnp.int32), axis=1) - 1


def head_grads(inputs):
    query_h, key_h, value_h, output_h, grad_h, lse_h, starts, block_list = inputs
    group_size = QH // KVH
    score_scale = HD ** -0.5
    positions = jnp.arange(SEQ, dtype=jnp.int32)
    docs = doc_index(starts, positions)
    query_tiles = query_h.astype(jnp.float32).reshape(NBLK, 128, group_size, HD)
    grad_tiles = grad_h.astype(jnp.float32).reshape(NBLK, 128, group_size, HD)
    output_tiles = output_h.astype(jnp.float32).reshape(NBLK, 128, group_size, HD)
    key_tiles = key_h.astype(jnp.float32).reshape(NBLK, 128, HD)
    value_tiles = value_h.astype(jnp.float32).reshape(NBLK, 128, HD)
    row_delta = jnp.transpose(jnp.sum(grad_tiles * output_tiles, axis=-1), (0, 2, 1))
    lse_tiles = jnp.transpose(lse_h.reshape(group_size, NBLK, 128), (1, 0, 2))
    doc_tiles = docs.reshape(NBLK, 128)
    pos_tiles = positions.reshape(NBLK, 128)
    grad_query = jnp.zeros((NBLK, 128, group_size, HD), jnp.float32)
    grad_key = jnp.zeros((NBLK, 128, HD), jnp.float32)
    grad_value = jnp.zeros((NBLK, 128, HD), jnp.float32)
    for entry_idx in range(KMAX):
        chosen = block_list[:, entry_idx]
        valid_rows = chosen >= 0
        picked = jnp.maximum(chosen, 0).astype(jnp.int32)
        key_sel = key_tiles[picked]
        value_sel = value_tiles[picked]
        allowed = valid_rows[:, None, None] & (doc_tiles[:, :, None] == doc_tiles[picked][:, None, :]) & (pos_tiles[:, :, None] >= pos_tiles[picked][:, None, :])
        scores = jnp.einsum('bird,bjd->brij', query_tiles, key_sel) * score_scale
        prob_full = jnp.where(allowed[:, None], jnp.exp(scores - lse_tiles[..., None]), 0.0)
        prob_half = lax.optimization_barrier(prob_full.astype(jnp.bfloat16)).astype(jnp.float32)
        dprobs = jnp.einsum('bird,bjd->brij', grad_tiles, value_sel)
        dscores = prob_full * (dprobs - row_delta[..., None]) * score_scale
        dscores = lax.optimization_barrier(dscores.astype(jnp.bfloat16)).astype(jnp.float32)
        grad_query = grad_query + jnp.einsum('brij,bjd->bird', dscores, key_sel)
        grad_key = grad_key.at[picked].add(jnp.einsum('brij,bird->bjd', dscores, query_tiles))
        grad_value = grad_value.at[picked].add(jnp.einsum('brij,bird->bjd', prob_half, grad_tiles))
    return (grad_query.reshape(SEQ, group_size * HD).astype(jnp.bfloat16),
            grad_key.reshape(SEQ, HD).astype(jnp.bfloat16),
            grad_value.reshape(SEQ, HD).astype(jnp.bfloat16))


def reference(features, queries, keys, values, attn_out, out_grad, lse, doc_starts, key_blocks):
    group_size = QH // KVH
    item_count = SECTIONS * KVH

    def split_query(array):
        return jnp.transpose(array.reshape(SECTIONS, SEQ, KVH, group_size, HD), (0, 2, 1, 3, 4)).reshape(item_count, SEQ, group_size, HD)

    def split_key(array):
        return jnp.transpose(array.reshape(SECTIONS, SEQ, KVH, HD), (0, 2, 1, 3)).reshape(item_count, SEQ, HD)

    starts_all = jnp.broadcast_to(doc_starts[:, None, :], (SECTIONS, KVH, DOC_CAP)).reshape(item_count, DOC_CAP)
    blocks_all = jnp.broadcast_to(key_blocks[:, None, :, :], (SECTIONS, KVH, NBLK, KMAX)).reshape(item_count, NBLK, KMAX)
    all_grads = lax.map(head_grads, (
        split_query(queries), split_key(keys), split_key(values),
        split_query(attn_out), split_query(out_grad),
        lse.reshape(item_count, group_size, SEQ),
        starts_all, blocks_all))
    grad_q = jnp.transpose(all_grads[0].reshape(SECTIONS, KVH, SEQ, group_size * HD), (0, 2, 1, 3)).reshape(SECTIONS, SEQ, QW)
    grad_k = jnp.transpose(all_grads[1].reshape(SECTIONS, KVH, SEQ, HD), (0, 2, 1, 3)).reshape(SECTIONS, SEQ, KVW)
    grad_v = jnp.transpose(all_grads[2].reshape(SECTIONS, KVH, SEQ, HD), (0, 2, 1, 3)).reshape(SECTIONS, SEQ, KVW)
    query_grad = jnp.roll(grad_q, -1, axis=0)
    key_grad = jnp.roll(grad_k, -1, axis=0)
    value_grad = jnp.roll(grad_v, -1, axis=0)
    weight_terms = []
    for section_idx in range(SECTIONS):
        total = lax.dot_general(features[section_idx], value_grad[section_idx], (((0,), (0,)), ((), ())), preferred_element_type=jnp.float32)
        weight_terms.append(total * (SEQ ** -0.5))
    return query_grad, key_grad, value_grad, jnp.stack(weight_terms)
```

```python
import functools

import jax
import jax.numpy as jnp
from jax import lax
from jax.experimental import pallas as pl
from jax.experimental.pallas import tpu as pltpu
from jax.sharding import PartitionSpec as P

QH = 64
KVH = 8
HD = 128
GROUP = QH // KVH
LOG2E = 1.4426950408889634
KT = 256
ROWS = 256
CHUNKS = GROUP * 128 // ROWS


def attn_kernel(bounds, q_ref, do_ref, lse_ref, delta_ref, beg_ref, k0, k1, k2, v0, v1, v2,
                dq_ref, dk_ref, dv_ref, kbuf, vbuf, dkacc, dvacc, qs, dos, dqacc):
    step = pl.program_id(0)
    tok = k0.shape[0]
    base = 2 * tok
    scale = HD ** -0.5

    @pl.when(step == 0)
    def _():
        for slot, (kr, vr) in enumerate(((k0, v0), (k1, v1), (k2, v2))):
            kbuf[slot * tok:(slot + 1) * tok, :] = kr[...]
            vbuf[slot * tok:(slot + 1) * tok, :] = vr[...]
        dkacc[...] = jnp.zeros_like(dkacc)
        dvacc[...] = jnp.zeros_like(dvacc)

    for h in range(GROUP):
        qs[h * 128:(h + 1) * 128, :] = q_ref[:, h * HD:(h + 1) * HD]
        dos[h * 128:(h + 1) * 128, :] = do_ref[:, h * HD:(h + 1) * HD]
    dqacc[...] = jnp.zeros_like(dqacc)

    lo = bounds[0, step]
    mid = bounds[1, step]
    last = bounds[2, step]
    row0 = base + step * 128

    def tile(pair, masked):
        start = pl.multiple_of(pair * KT, KT)
        k = kbuf[pl.ds(start, KT), :]
        v = vbuf[pl.ds(start, KT), :]
        if masked:
            u = lax.broadcasted_iota(jnp.int32, (KT, ROWS), 0) + start
            t = (lax.broadcasted_iota(jnp.int32, (1, ROWS), 1) & 127) + row0
            allowed = (u >= beg_ref[0]) & (u <= t)
        dk = None
        dv = None
        for c in range(CHUNKS):
            at = slice(c * ROWS, (c + 1) * ROWS)
            q = qs[at, :]
            g = dos[at, :]
            s = lax.dot_general(k, q, (((1,), (1,)), ((), ())), preferred_element_type=jnp.float32)
            p = jnp.exp2(s * (scale * LOG2E) - lse_ref[0, 0, c:c + 1, :])
            if masked:
                p = jnp.where(allowed, p, 0.0)
            dp = lax.dot_general(v, g, (((1,), (1,)), ((), ())), preferred_element_type=jnp.float32)
            ds = (p * (dp - delta_ref[0, 0, c:c + 1, :])).astype(jnp.bfloat16)
            pb = p.astype(jnp.bfloat16)
            dvc = jnp.dot(pb, g, preferred_element_type=jnp.float32)
            dkc = jnp.dot(ds, q, preferred_element_type=jnp.float32)
            dk = dkc if dk is None else dk + dkc
            dv = dvc if dv is None else dv + dvc
            dqacc[at, :] += lax.dot_general(ds, k, (((0,), (0,)), ((), ())), preferred_element_type=jnp.float32)
        dkacc[pl.ds(start, KT), :] += dk
        dvacc[pl.ds(start, KT), :] += dv

    edge = mid - lo

    def masked_step(i, carry):
        tile(jnp.where(i < edge, lo + i, last), True)
        return carry

    def plain_step(i, carry):
        tile(i, False)
        return carry

    lax.fori_loop(0, edge + 1, masked_step, 0)
    lax.fori_loop(mid, last, plain_step, 0)

    for h in range(GROUP):
        dq_ref[:, h * HD:(h + 1) * HD] = (dqacc[h * 128:(h + 1) * 128, :] * scale).astype(jnp.bfloat16)

    @pl.when(step == pl.num_programs(0) - 1)
    def _():
        for slot in range(3):
            dk_ref[slot] = (dkacc[slot * tok:(slot + 1) * tok, :] * scale).astype(jnp.bfloat16)
            dv_ref[slot] = dvacc[slot * tok:(slot + 1) * tok, :].astype(jnp.bfloat16)


def attention(head, bounds, q, do, lse, delta, beg, ks, vs):
    tok = q.shape[0]
    blocks = tok // 128
    width = GROUP * HD
    spec_q = pl.BlockSpec((128, width), lambda i, *_: (i, head))
    spec_row = pl.BlockSpec((1, 1, CHUNKS, ROWS), lambda i, *_: (head, i, 0, 0))
    spec_kv = pl.BlockSpec((tok, HD), lambda i, *_: (0, head))
    spec_grad = pl.BlockSpec((3, tok, HD), lambda i, *_: (0, 0, 0))
    pairs = blocks * 11 // 2
    return pl.pallas_call(
        attn_kernel,
        out_shape=(
            jax.ShapeDtypeStruct((tok, width), jnp.bfloat16),
            jax.ShapeDtypeStruct((3, tok, HD), jnp.bfloat16),
            jax.ShapeDtypeStruct((3, tok, HD), jnp.bfloat16),
        ),
        grid_spec=pltpu.PrefetchScalarGridSpec(
            num_scalar_prefetch=1,
            grid=(blocks,),
            in_specs=[spec_q, spec_q, spec_row, spec_row,
                      pl.BlockSpec((1, 1, ROWS), lambda i, *_: (i, 0, 0))] + [spec_kv] * 6,
            out_specs=[pl.BlockSpec((128, width), lambda i, *_: (i, 0)), spec_grad, spec_grad],
            scratch_shapes=[
                pltpu.VMEM((3 * tok, HD), jnp.bfloat16),
                pltpu.VMEM((3 * tok, HD), jnp.bfloat16),
                pltpu.VMEM((3 * tok, HD), jnp.float32),
                pltpu.VMEM((3 * tok, HD), jnp.float32),
                pltpu.VMEM((width, HD), jnp.bfloat16),
                pltpu.VMEM((width, HD), jnp.bfloat16),
                pltpu.VMEM((width, HD), jnp.float32),
            ],
        ),
        compiler_params=pltpu.CompilerParams(
            dimension_semantics=("arbitrary",), vmem_limit_bytes=40 << 20),
        cost_estimate=pl.CostEstimate(
            flops=pairs * 10 * KT * width * HD, transcendentals=pairs * KT * width,
            bytes_accessed=10 << 20),
        name="attn_grad",
    )(bounds, q, do, lse, delta, beg, *ks, *vs)


def block_tables(starts, shard, tok):
    blocks = tok // 128
    pos = shard * tok + jnp.arange(tok, dtype=jnp.int32)
    begin = jnp.max(jnp.where(starts[None, :] <= pos[:, None], starts[None, :], 0), axis=1)
    begin = (begin - (shard - 2) * tok).reshape(blocks, 128)
    last = (2 * tok // 128 + jnp.arange(blocks, dtype=jnp.int32)) * 128 // KT
    lo = begin[:, 0] // KT
    mid = jnp.minimum((begin[:, -1] + KT - 1) // KT, last)
    beg = jnp.tile(begin, (1, ROWS // 128)).reshape(blocks, 1, ROWS)
    return jnp.stack([lo, mid, last]).astype(jnp.int32), beg


def row_tables(array, kv_local):
    blocks = array.shape[1] // 128
    grid = array.reshape(kv_local, CHUNKS, ROWS // 128, blocks, 128)
    return jnp.transpose(grid, (0, 3, 1, 2, 4)).reshape(kv_local, blocks, CHUNKS, ROWS)


def ctx_send(array, by):
    n = lax.axis_size("ctx")
    return lax.ppermute(array, "ctx", [(i, i + by) for i in range(n) if 0 <= i + by < n])


def home(array, by):
    n = lax.axis_size("ctx")
    m = lax.axis_size("section")
    pairs = [(s * n + i, (s - 1) % m * n + i - by)
             for s in range(m) for i in range(n) if i - by >= 0]
    return lax.ppermute(array, ("section", "ctx"), pairs)


def local(features, queries, keys, values, attn_out, out_grad, lse, doc_starts, key_blocks):
    tok = queries.shape[1]
    kv_local = keys.shape[2] // HD
    shard = lax.axis_index("ctx")
    ctx = lax.axis_size("ctx")
    dp = lax.axis_size("dp")
    own_k, own_v = keys[0], values[0]
    k1, v1 = ctx_send((own_k, own_v), 1)
    k0, v0 = ctx_send((own_k, own_v), 2)
    bounds, beg = block_tables(doc_starts[0], shard, tok)
    delta = jnp.einsum(
        "igd,igd->gi",
        out_grad[0].astype(jnp.float32).reshape(tok, kv_local * GROUP, HD),
        attn_out[0].astype(jnp.float32).reshape(tok, kv_local * GROUP, HD))
    delta = row_tables(delta, kv_local)
    lse2 = row_tables(lse[0] * LOG2E, kv_local)
    feat = features[0]
    scale = (tok * ctx) ** -0.5
    rows = feat.shape[1] // ctx
    dq_parts, dk_parts, dv_parts, w_parts = [], [], [], []
    for head in range(kv_local):
        dq, dk, dv = attention(head, bounds, queries[0], out_grad[0], lse2, delta, beg,
                               (k0, k1, own_k), (v0, v1, own_v))
        dv_sum = home(dv[2], 0).astype(jnp.float32) + home(dv[1], 1) + home(dv[0], 2)
        dv_sum = dv_sum.astype(jnp.bfloat16)
        dv_all = lax.all_gather(dv_sum, "dp", axis=1, tiled=True)
        dk_sum = home(dk[2], 0).astype(jnp.float32) + home(dk[1], 1) + home(dk[0], 2)
        dq_parts.append(home(dq, 0))
        dk_parts.append(dk_sum.astype(jnp.bfloat16))
        dv_parts.append(dv_sum)

        def partial(target):
            cols = lax.dynamic_slice_in_dim(feat, target * rows, rows, 1)
            return lax.dot_general(cols, dv_all, (((0,), (0,)), ((), ())),
                                   preferred_element_type=jnp.float32)

        total = partial(shard)
        for by in range(1, ctx):
            sent = partial((shard + by) % ctx).astype(jnp.bfloat16)
            total = total + lax.ppermute(sent, "ctx", [(i, (i + by) % ctx) for i in range(ctx)])
        w_parts.append((total * scale).reshape(rows, dp, 1, HD))
    weight = jnp.concatenate(w_parts, axis=2).reshape(rows, dp * kv_local * HD)
    return (jnp.concatenate(dq_parts, axis=1)[None],
            jnp.concatenate(dk_parts, axis=1)[None],
            jnp.concatenate(dv_parts, axis=1)[None],
            weight[None])


def solution(mesh):
    placed = (
        P("section", "ctx", "dp"),
        P("section", "ctx", "dp"),
        P("section", "ctx", "dp"),
        P("section", "ctx", "dp"),
        P("section", "ctx", "dp"),
        P("section", "ctx", "dp"),
        P("section", "dp", "ctx"),
        P("section", None),
        P("section", "ctx", None),
    )
    return jax.shard_map(
        local,
        mesh=mesh,
        in_specs=placed,
        out_specs=(
            P("section", "ctx", "dp"),
            P("section", "ctx", "dp"),
            P("section", "ctx", "dp"),
            P("section", ("dp", "ctx"), None),
        ),
        check_vma=False,
    )
```

```python
import functools

import jax
import jax.numpy as jnp
from jax import lax
from jax.experimental import pallas as pl
from jax.experimental.pallas import tpu as pltpu
from jax.sharding import PartitionSpec as P

QH = 64
KVH = 8
HD = 128
GROUP = QH // KVH
LOG2E = 1.4426950408889634
KT = 256
ROWS = 1024
CHUNKS = GROUP * 128 // ROWS


def attn_kernel(bounds, q_ref, do_ref, lse_ref, delta_ref, beg_ref, k0, k1, k2, v0, v1, v2,
                dq_ref, dk_ref, dv_ref, kbuf, vbuf, dkacc, dvacc, qs, dos, dqacc):
    step = pl.program_id(0)
    tok = k0.shape[0]
    base = 2 * tok
    scale = HD ** -0.5

    @pl.when(step == 0)
    def _():
        for slot, (kr, vr) in enumerate(((k0, v0), (k1, v1), (k2, v2))):
            kbuf[slot * tok:(slot + 1) * tok, :] = kr[...]
            vbuf[slot * tok:(slot + 1) * tok, :] = vr[...]
        dkacc[...] = jnp.zeros_like(dkacc)
        dvacc[...] = jnp.zeros_like(dvacc)

    for h in range(GROUP):
        qs[h * 128:(h + 1) * 128, :] = q_ref[:, h * HD:(h + 1) * HD]
        dos[h * 128:(h + 1) * 128, :] = do_ref[:, h * HD:(h + 1) * HD]
    dqacc[...] = jnp.zeros_like(dqacc)

    lo = bounds[0, step]
    mid = bounds[1, step]
    last = bounds[2, step]
    row0 = base + step * 128

    def tile(pair, masked):
        start = pl.multiple_of(pair * KT, KT)
        k = kbuf[pl.ds(start, KT), :]
        kt = k.T
        v = vbuf[pl.ds(start, KT), :]
        if masked:
            u = lax.broadcasted_iota(jnp.int32, (KT, ROWS), 0) + start
            t = (lax.broadcasted_iota(jnp.int32, (1, ROWS), 1) & 127) + row0
            allowed = (u >= beg_ref[0]) & (u <= t)
        dk = None
        dv = None
        for c in range(CHUNKS):
            at = slice(c * ROWS, (c + 1) * ROWS)
            q = qs[at, :]
            g = dos[at, :]
            s = lax.dot_general(k, q, (((1,), (1,)), ((), ())), preferred_element_type=jnp.float32)
            p = jnp.exp2(s * (scale * LOG2E) - lse_ref[0, 0, c:c + 1, :])
            if masked:
                p = jnp.where(allowed, p, 0.0)
            dp = lax.dot_general(v, g, (((1,), (1,)), ((), ())), preferred_element_type=jnp.float32)
            ds = (p * (dp - delta_ref[0, 0, c:c + 1, :])).astype(jnp.bfloat16)
            pb = p.astype(jnp.bfloat16)
            dvc = jnp.dot(pb, g, preferred_element_type=jnp.float32)
            dkc = jnp.dot(ds, q, preferred_element_type=jnp.float32)
            dk = dkc if dk is None else dk + dkc
            dv = dvc if dv is None else dv + dvc
            dqacc[:, at] += jnp.dot(kt, ds, preferred_element_type=jnp.float32)
        dkacc[pl.ds(start, KT), :] += dk
        dvacc[pl.ds(start, KT), :] += dv

    edge = mid - lo

    def masked_step(i, carry):
        tile(jnp.where(i < edge, lo + i, last), True)
        return carry

    def plain_step(i, carry):
        tile(i, False)
        return carry

    lax.fori_loop(0, edge + 1, masked_step, 0)
    lax.fori_loop(mid, last, plain_step, 0)

    for h in range(GROUP):
        dq_ref[:, h * HD:(h + 1) * HD] = (dqacc[:, h * 128:(h + 1) * 128].T * scale).astype(jnp.bfloat16)

    @pl.when(step == pl.num_programs(0) - 1)
    def _():
        for slot in range(3):
            dk_ref[slot] = (dkacc[slot * tok:(slot + 1) * tok, :] * scale).astype(jnp.bfloat16)
            dv_ref[slot] = dvacc[slot * tok:(slot + 1) * tok, :].astype(jnp.bfloat16)


def attention(head, bounds, q, do, lse, delta, beg, ks, vs):
    tok = q.shape[0]
    blocks = tok // 128
    width = GROUP * HD
    spec_q = pl.BlockSpec((128, width), lambda i, *_: (i, head))
    spec_row = pl.BlockSpec((1, 1, CHUNKS, ROWS), lambda i, *_: (head, i, 0, 0))
    spec_kv = pl.BlockSpec((tok, HD), lambda i, *_: (0, 0))
    spec_grad = pl.BlockSpec((3, tok, HD), lambda i, *_: (0, 0, 0))
    pairs = blocks * 11 // 2
    return pl.pallas_call(
        attn_kernel,
        out_shape=(
            jax.ShapeDtypeStruct((tok, width), jnp.bfloat16),
            jax.ShapeDtypeStruct((3, tok, HD), jnp.bfloat16),
            jax.ShapeDtypeStruct((3, tok, HD), jnp.bfloat16),
        ),
        grid_spec=pltpu.PrefetchScalarGridSpec(
            num_scalar_prefetch=1,
            grid=(blocks,),
            in_specs=[spec_q, spec_q, spec_row, spec_row,
                      pl.BlockSpec((1, 1, ROWS), lambda i, *_: (i, 0, 0))] + [spec_kv] * 6,
            out_specs=[pl.BlockSpec((128, width), lambda i, *_: (i, 0)), spec_grad, spec_grad],
            scratch_shapes=[
                pltpu.VMEM((3 * tok, HD), jnp.bfloat16),
                pltpu.VMEM((3 * tok, HD), jnp.bfloat16),
                pltpu.VMEM((3 * tok, HD), jnp.float32),
                pltpu.VMEM((3 * tok, HD), jnp.float32),
                pltpu.VMEM((width, HD), jnp.bfloat16),
                pltpu.VMEM((width, HD), jnp.bfloat16),
                pltpu.VMEM((HD, width), jnp.float32),
            ],
        ),
        compiler_params=pltpu.CompilerParams(
            dimension_semantics=("arbitrary",), vmem_limit_bytes=40 << 20),
        cost_estimate=pl.CostEstimate(
            flops=pairs * 10 * KT * width * HD, transcendentals=pairs * KT * width,
            bytes_accessed=10 << 20),
        name="attn_grad",
    )(bounds, q, do, lse, delta, beg, *ks, *vs)


def block_tables(starts, shard, tok):
    blocks = tok // 128
    pos = shard * tok + jnp.arange(tok, dtype=jnp.int32)
    begin = jnp.max(jnp.where(starts[None, :] <= pos[:, None], starts[None, :], 0), axis=1)
    begin = (begin - (shard - 2) * tok).reshape(blocks, 128)
    last = (2 * tok // 128 + jnp.arange(blocks, dtype=jnp.int32)) * 128 // KT
    lo = begin[:, 0] // KT
    mid = jnp.minimum((begin[:, -1] + KT - 1) // KT, last)
    beg = jnp.tile(begin, (1, ROWS // 128)).reshape(blocks, 1, ROWS)
    return jnp.stack([lo, mid, last]).astype(jnp.int32), beg


def row_tables(array, kv_local):
    blocks = array.shape[1] // 128
    grid = array.reshape(kv_local, CHUNKS, ROWS // 128, blocks, 128)
    return jnp.transpose(grid, (0, 3, 1, 2, 4)).reshape(kv_local, blocks, CHUNKS, ROWS)


def ctx_send(array, by):
    n = lax.axis_size("ctx")
    return lax.ppermute(array, "ctx", [(i, i + by) for i in range(n) if 0 <= i + by < n])


def home(array, by):
    n = lax.axis_size("ctx")
    m = lax.axis_size("section")
    pairs = [(s * n + i, (s - 1) % m * n + i - by)
             for s in range(m) for i in range(n) if i - by >= 0]
    return lax.ppermute(array, ("section", "ctx"), pairs)


def local(features, queries, keys, values, attn_out, out_grad, lse, doc_starts, key_blocks):
    tok = queries.shape[1]
    kv_local = keys.shape[2] // HD
    shard = lax.axis_index("ctx")
    ctx = lax.axis_size("ctx")
    dp = lax.axis_size("dp")
    own_k, own_v = keys[0], values[0]
    windows = []
    for head in range(kv_local):
        own = [a[:, head * HD:(head + 1) * HD] for a in (own_k, own_v)]
        windows.append((ctx_send(own, 2), ctx_send(own, 1), own))
    bounds, beg = block_tables(doc_starts[0], shard, tok)
    delta = jnp.einsum(
        "igd,igd->gi",
        out_grad[0].astype(jnp.float32).reshape(tok, kv_local * GROUP, HD),
        attn_out[0].astype(jnp.float32).reshape(tok, kv_local * GROUP, HD))
    delta = row_tables(delta, kv_local)
    lse2 = row_tables(lse[0] * LOG2E, kv_local)
    feat = features[0]
    scale = (tok * ctx) ** -0.5
    rows = feat.shape[1] // ctx
    dq_parts, dk_parts, dv_parts, w_parts = [], [], [], []
    for head in range(kv_local):
        dq, dk, dv = attention(head, bounds, queries[0], out_grad[0], lse2, delta, beg,
                               [slot[0] for slot in windows[head]],
                               [slot[1] for slot in windows[head]])
        dv_sum = home(dv[2], 0).astype(jnp.float32) + home(dv[1], 1) + home(dv[0], 2)
        dv_sum = dv_sum.astype(jnp.bfloat16)
        dv_all = lax.all_gather(dv_sum, "dp", axis=1, tiled=True)
        dk_sum = home(dk[2], 0).astype(jnp.float32) + home(dk[1], 1) + home(dk[0], 2)
        dq_parts.append(home(dq, 0))
        dk_parts.append(dk_sum.astype(jnp.bfloat16))
        dv_parts.append(dv_sum)

        def partial(target):
            cols = lax.dynamic_slice_in_dim(feat, target * rows, rows, 1)
            return lax.dot_general(cols, dv_all, (((0,), (0,)), ((), ())),
                                   preferred_element_type=jnp.float32)

        total = partial(shard)
        for by in range(1, ctx):
            sent = partial((shard + by) % ctx).astype(jnp.bfloat16)
            total = total + lax.ppermute(sent, "ctx", [(i, (i + by) % ctx) for i in range(ctx)])
        w_parts.append((total * scale).reshape(rows, dp, 1, HD))
    weight = jnp.concatenate(w_parts, axis=2).reshape(rows, dp * kv_local * HD)
    return (jnp.concatenate(dq_parts, axis=1)[None],
            jnp.concatenate(dk_parts, axis=1)[None],
            jnp.concatenate(dv_parts, axis=1)[None],
            weight[None])


def solution(mesh):
    placed = (
        P("section", "ctx", "dp"),
        P("section", "ctx", "dp"),
        P("section", "ctx", "dp"),
        P("section", "ctx", "dp"),
        P("section", "ctx", "dp"),
        P("section", "ctx", "dp"),
        P("section", "dp", "ctx"),
        P("section", None),
        P("section", "ctx", None),
    )
    return jax.shard_map(
        local,
        mesh=mesh,
        in_specs=placed,
        out_specs=(
            P("section", "ctx", "dp"),
            P("section", "ctx", "dp"),
            P("section", "ctx", "dp"),
            P("section", ("dp", "ctx"), None),
        ),
        check_vma=False,
    )
```
